32 devices in a mesh: row: 8 (over z, core), col: 4 (over y, x).
Axes of the slice: x: 2, y: 2, z: 4, core: 2. Of those that a mesh axis runs over, the one named last changes fastest.
Arguments:
- radar_field: float32 [64, 64, 384], P('row', 'col'), may hold values from -6 to 6
- kernels: bfloat16 [2, 2, 3, 3, 384, 384], P(None, None, None, None, None, 'row'), may hold values from -0.109375 to 0.109375
- norm_gain_weights: float32 [2, 384], replicated, may hold values from 0.25 to 1.75
Outputs:
- field_out: float32 [64, 64, 384], P('row', 'col')
The draws below stay inside these ranges and needn't reach their ends.
All inputs are finite; a program needn't handle non-finite values.
Results may differ from the reference program's by a relative error of at most 0.0032.
Values may be sent and summed in bfloat16 or wider, within the bound.
A program may use at most 64 MiB of HBM per device.

```python
import jax
import jax.numpy as jnp
from jax import lax

C = 384
BLOCKS = 2
FIRST_DILATION = 32
SECOND_DILATION = 64
H = 64
W = 64


def level_of(rng, dims, cuts, low, high):
    def one(axis_at, shards_of):
        draws = jax.random.uniform(jax.random.fold_in(jax.random.fold_in(rng, 6), axis_at), (shards_of,), jnp.float32, low / len(cuts), high / len(cuts))
        return jnp.repeat(jnp.exp(draws), dims[axis_at] // shards_of).reshape((-1,) + (1,) * (len(dims) - axis_at - 1))

    factor_of = one(*cuts[0])
    for cut in cuts[1:]:
        factor_of = factor_of * one(*cut)
    return factor_of


def scatter_about(own_key, dims, deviation, reach, shards=(), dtype=jnp.bfloat16):
    gain = level_of(own_key, dims, shards, -0.22, 0.18) if shards else 1.0
    entries = jax.random.normal(own_key, dims, jnp.float32) * deviation * gain
    return jnp.minimum(jnp.maximum(entries, -reach), reach).astype(dtype)


def setup_inputs(seed: int = 0) -> dict:
    key_of = jax.random.split(jax.random.key(seed), 4)
    radar_field = scatter_about(key_of[0], (H, W, C), 1.0, 6.0, ((0, 8), (1, 4)), jnp.float32)
    kernels = scatter_about(key_of[1], (BLOCKS, 2, 3, 3, C, C), (9 * C) ** -0.5, 0.109375, ((5, 8),))
    norm_gain_weights = jnp.clip(1.0 + 0.15 * jax.random.normal(key_of[2], (BLOCKS, C), jnp.float32), 0.25, 1.75)
    return dict(radar_field=radar_field, kernels=kernels, norm_gain_weights=norm_gain_weights)


norm_floor = 1e-06

def convolve(image, kernel, dilation):
    result = lax.conv_general_dilated(image[None], kernel, (1, 1), ((dilation, dilation), (dilation, dilation)), rhs_dilation=(dilation, dilation), dimension_numbers=('NHWC', 'HWIO', 'NHWC'), preferred_element_type=jnp.float32)
    return result[0]

def reference(radar_field, kernels, norm_gain_weights):
    current = radar_field
    dilation_list = [FIRST_DILATION, SECOND_DILATION]
    for block_index in range(BLOCKS):
        cast_state = current.astype(jnp.bfloat16)
        dilated_output = convolve(cast_state, kernels[block_index, 0], dilation_list[block_index])
        mean_square = lax.optimization_barrier(jnp.mean(dilated_output * dilated_output, axis=-1, keepdims=True))
        normed = dilated_output / jnp.sqrt(mean_square + norm_floor) * norm_gain_weights[block_index]
        hidden = jax.nn.relu(normed).astype(jnp.bfloat16)
        plain = convolve(hidden, kernels[block_index, 1], 1)
        current = current + plain
    return current
```

```python
import functools

import jax
import jax.numpy as jnp
from jax import lax
from jax.experimental import pallas as pl
from jax.experimental.pallas import tpu as pltpu
from jax.sharding import PartitionSpec as P

BLOCKS = 2
FIRST_DILATION = 32
SECOND_DILATION = 64


norm_floor = 1e-06


def passed_along(value, axis, steps):
    count = lax.axis_size(axis)
    initial, last = (max(0, -steps), min(count, count - steps))
    return lax.ppermute(value, axis, [(source, source + steps) for source in range(initial, last)])


def extended(cells, sides, width):
    for axis, dim in sides:
        count = lax.axis_size(axis)
        ends = count - 1
        head = lax.slice_in_dim(cells, 0, width, axis=dim)
        tail = lax.slice_in_dim(cells, cells.shape[dim] - width, cells.shape[dim], axis=dim)
        cells = jnp.concatenate(
            [
                lax.ppermute(tail, axis, [(i, (i + 1) % count) for i in range(ends)]),
                cells,
                lax.ppermute(head, axis, [((i + 1) % count, i) for i in range(ends)]),
            ],
            axis=dim,
        )
    return cells


def row_direction(stacked, tap_displacement):
    moved = {}
    for side in (-1, 1):
        moved[side] = passed_along(stacked, "row", -side * tap_displacement)
    return moved


def along_cols(stacked, tap_displacement):
    moved = {}
    for side in (-1, 1):
        moved[side] = passed_along(stacked, "col", -side * tap_displacement)
    return moved


def dilated_taps(cast_state, row_step, col_step):
    tap_list = []
    row_moved = row_direction(cast_state, row_step)
    centre = jnp.stack([row_moved[-1], cast_state, row_moved[1]])
    col_moved = along_cols(centre, col_step)
    for row_off in (-1, 0, 1):
        for col_off in (-1, 0, 1):
            if col_off == 0:
                tap_list.append(centre[row_off + 1])
            else:
                tap_list.append(col_moved[col_off][row_off + 1])
    return jnp.stack(tap_list)


def contract(tap_stack, kernel_part):
    channels = tap_stack.shape[-1]
    flat_taps = tap_stack.reshape(9, -1, channels)
    flat_kernel = kernel_part.reshape(9, channels, -1)
    return lax.dot_general(
        flat_taps, flat_kernel, (((0, 2), (0, 1)), ((), ())), preferred_element_type=jnp.float32
    )


def convolve(tap_stack, kernels, block_index, which):
    gathered = lax.all_gather(kernels[block_index, which], "row", axis=3, tiled=True)
    return contract(tap_stack, gathered)


def per_device(radar_field, kernels, norm_gain_weights):
    tile_rows, tile_cols, channels = radar_field.shape
    dilation_list = [FIRST_DILATION, SECOND_DILATION]
    current = radar_field
    for block_index in range(BLOCKS):
        cast_state = current.astype(jnp.bfloat16)
        spacing = dilation_list[block_index]
        tap_stack = dilated_taps(cast_state, spacing // tile_rows, spacing // tile_cols)
        dilated_output = convolve(tap_stack, kernels, block_index, 0)
        mean_square = jnp.mean(dilated_output * dilated_output, axis=-1, keepdims=True)
        normed = (
            dilated_output / jnp.sqrt(mean_square + norm_floor) * norm_gain_weights[block_index]
        )
        hidden = jax.nn.relu(normed).astype(jnp.bfloat16).reshape(tile_rows, tile_cols, channels)
        padded = extended(hidden, (("row", 0), ("col", 1)), 1)
        plain_taps = []
        for row_off in range(3):
            for col_off in range(3):
                plain_taps.append(
                    padded[row_off : row_off + tile_rows, col_off : col_off + tile_cols]
                )
        plain = convolve(jnp.stack(plain_taps), kernels, block_index, 1)
        current = current + plain.reshape(tile_rows, tile_cols, channels)
    return current


MESH = pl.DeviceIdType.MESH
PLANE = 4


def fits(rows, cols, tile, shard):
    height, width = rows * tile[0], cols * tile[1]
    return (
        cols == PLANE
        and rows % 4 == 0
        and height == 2 * FIRST_DILATION
        and width == 2 * FIRST_DILATION
        and SECOND_DILATION >= max(height, width)
        and shard[-1] % 16 == 0
        and tile[1] % 16 == 0
    )


def block_kernel(
    rows, cols, th, tw, taps,
    x_ref, w_ref, radar_ref, gain_ref, o_ref,
    wg, xin, hs, ce, rowhalo, colhalo, hp, current,
    local_sem, w_recv, up_send, down_send, x_send, y_send, diag_send, core_send, core_recv,
    tile_send, tile_recv, halo_send, halo_recv,
):
    row, col = lax.axis_index("row"), lax.axis_index("col")
    depth = rows // 2
    groups = taps // cols
    z, core = row // 2, row % 2
    channels = x_ref.shape[-1]
    col_of = [col, col + 1 - 2 * (col % 2), (col + 2) % 4, 3 - col]
    other_core = row + 1 - 2 * core
    far_row = (row + depth) % rows
    far_col = col_of[2]

    def remote(source, target, send, recv, to_row, to_col):
        return pltpu.make_async_remote_copy(
            src_ref=source,
            dst_ref=target,
            send_sem=send,
            recv_sem=recv,
            device_id={"row": to_row, "col": to_col},
            device_id_type=MESH,
        )

    for g in range(groups):
        span = pl.ds(g * cols, cols)
        pltpu.make_async_copy(w_ref.at[span], wg.at[span, z, core], local_sem.at[g]).start()

    neighbours = []
    for dr in (-1, 0, 1):
        for dc in (-1, 0, 1):
            if dr or dc:
                ok = (row + dr >= 0) & (row + dr < rows) & (col + dc >= 0) & (col + dc < cols)
                neighbours.append((dr, dc, ok))

    barrier = pltpu.get_barrier_semaphore()
    greeted = [
        (z > 0, row - 2, col),
        (z < depth - 1, row + 2, col),
        (None, row, col_of[1]),
        (None, row, col_of[2]),
        (None, other_core, col),
        (None, far_row, col),
    ] + [(ok, row + dr, col + dc) for dr, dc, ok in neighbours]
    expected = 0
    for ok, to_row, to_col in greeted:
        def greet(to_row=to_row, to_col=to_col):
            pl.semaphore_signal(barrier, inc=1, device_id={"row": to_row, "col": to_col}, device_id_type=MESH)

        if ok is None:
            greet()
            expected = expected + 1
        else:
            pl.when(ok)(greet)
            expected = expected + jnp.where(ok, 1, 0)
    hp[...] = jnp.zeros_like(hp)
    for g in range(groups):
        span = pl.ds(g * cols, cols)
        pltpu.make_async_copy(w_ref.at[span], wg.at[span, z, core], local_sem.at[g]).wait()
    pl.semaphore_wait(barrier, expected)

    def piece(g, j, source):
        return wg.at[cols * g + col_of[j], source, core]

    def z_up(g, source):
        p = piece(g, 0, source)
        return remote(p, p, up_send.at[g, source], w_recv.at[g, 0, source], row + 2, col)

    def z_down(g, source):
        p = piece(g, 0, source)
        return remote(p, p, down_send.at[g, source], w_recv.at[g, 0, source], row - 2, col)

    def to_x(g, source):
        p = piece(g, 0, source)
        return remote(p, p, x_send.at[g, source], w_recv.at[g, 1, source], row, col_of[1])

    def to_y(g, source):
        p = piece(g, 0, source)
        return remote(p, p, y_send.at[g, source], w_recv.at[g, 2, source], row, col_of[2])

    def relay_via(g):
        return 1 if g % 3 == 0 else 2

    def to_diag(g, source):
        via = relay_via(g)
        p = piece(g, via, source)
        return remote(p, p, diag_send.at[g, source], w_recv.at[g, 3, source], row, col_of[3 - via])

    def to_core(g, j):
        p = wg.at[cols * g + col_of[j], :, core]
        return remote(p, p, core_send.at[g, j], core_recv.at[g, j], other_core, col)

    def from_core(g, j):
        p = wg.at[cols * g + col_of[j], :, 1 - core]
        return remote(p, p, core_send.at[g, j], core_recv.at[g, j], other_core, col)

    def arrived(g, j, source):
        p = piece(g, j, source)
        remote(p, p, x_send.at[g, source], w_recv.at[g, j, source], row, col_of[1]).wait_recv()

    def others(act):
        for d in range(1, depth):
            for side in (-1, 1):
                source = z + side * d
                pl.when((source >= 0) & (source < depth))(functools.partial(act, source, side, d))

    def own_z(g):
        pl.when(z < depth - 1)(lambda: z_up(g, z).start())
        pl.when(z > 0)(lambda: z_down(g, z).start())

    def z_phase(g):
        def act(source, side, d):
            arrived(g, 0, source)
            if side < 0:
                pl.when(z < depth - 1)(lambda: z_up(g, source).start())
            else:
                pl.when(z > 0)(lambda: z_down(g, source).start())
            to_x(g, source).start()
            to_y(g, source).start()

        others(act)
        to_core(g, 0).start()

    def plane_phase(g):
        via = relay_via(g)

        def act(source, side, d):
            arrived(g, via, source)
            to_diag(g, source).start()
            arrived(g, 3 - via, source)

        others(act)
        to_core(g, 1).start()
        to_core(g, 2).start()

    def diag_phase(g):
        others(lambda source, side, d: arrived(g, 3, source))
        to_core(g, 3).start()

    def core_phase(g):
        for j in range(4):
            from_core(g, j).wait_recv()

    tile_copies = [
        remote(x_ref, xin.at[0], tile_send.at[0], tile_recv.at[0], far_row, col),
        remote(x_ref, xin.at[1], tile_send.at[1], tile_recv.at[1], row, far_col),
        remote(xin.at[0], xin.at[2], tile_send.at[2], tile_recv.at[2], row, far_col),
    ]

    def product(cells, tap):
        weight = wg[tap].reshape(channels, channels)
        return lax.dot_general(cells, weight, (((1,), (1,)), ((), ())), preferred_element_type=jnp.float32)

    def halo_copy(b, n):
        dr, dc, _ = neighbours[n]
        if dc == 0:
            source = hs.at[b, 0 if dr < 0 else th - 1]
            target = rowhalo.at[b, 1 if dr < 0 else 0]
        else:
            source = ce.at[b, 0 if dc < 0 else 1]
            target = colhalo.at[b, 1 if dc < 0 else 0, 1 - dr]
        return remote(source, target, halo_send.at[b, n], halo_recv.at[b, 7 - n], row + dr, col + dc)

    def halo_arrived(b, n):
        dr, dc, _ = neighbours[n]
        if dc == 0:
            target = rowhalo.at[b, 0 if dr < 0 else 1]
        else:
            target = colhalo.at[b, 0 if dc < 0 else 1, dr + 1]
        remote(target, target, halo_send.at[b, n], halo_recv.at[b, n], row + dr, col + dc).wait_recv()

    def normalize(b, dilated):
        mean_square = jnp.mean(dilated * dilated, axis=-1, keepdims=True)
        normed = dilated / jnp.sqrt(mean_square + norm_floor) * gain_ref[b : b + 1, :]
        hidden = jax.nn.relu(normed).astype(jnp.bfloat16).reshape(th, tw, channels)
        hs[b] = hidden
        wide = hidden.astype(jnp.float32)
        ce[b, 0] = wide[:, 0, :].astype(jnp.bfloat16)
        ce[b, 1] = wide[:, tw - 1, :].astype(jnp.bfloat16)
        hp[1 : th + 1, 1 : tw + 1, :] = wide
        for n, (dr, dc, ok) in enumerate(neighbours):
            pl.when(ok)(lambda n=n: halo_copy(b, n).start())

    def take_halo(b):
        for n, (dr, dc, ok) in enumerate(neighbours):
            def act(n=n, dr=dr, dc=dc):
                halo_arrived(b, n)
                to_row = 0 if dr < 0 else th + 1
                to_col = 0 if dc < 0 else tw + 1
                if dc == 0:
                    hp[to_row, 1 : tw + 1, :] = rowhalo[b, 0 if dr < 0 else 1].astype(jnp.float32)
                else:
                    edge = colhalo[b, 0 if dc < 0 else 1, dr + 1].astype(jnp.float32)
                    if dr == 0:
                        hp[1 : th + 1, to_col : to_col + 1, :] = edge.reshape(th, 1, channels)
                    else:
                        at = th - 1 if dr < 0 else 0
                        hp[to_row, to_col : to_col + 1, :] = edge[at : at + 1, :]

            pl.when(ok)(act)

    def shifted(tap):
        p, q = tap // 3, tap % 3
        return hp[p : p + th, q : q + tw, :].astype(jnp.bfloat16).reshape(th * tw, channels)

    def first_block():
        tile_copies[1].wait_recv()
        tile_copies[2].wait_recv()
        far_p = jnp.where(row < depth, 2, 0)
        far_q = jnp.where(col < cols // 2, 2, 0)
        dilated = product(x_ref[...], 4)
        dilated += product(xin[0], far_p * 3 + 1)
        dilated += product(xin[1], 3 + far_q)
        dilated += product(xin[2], far_p * 3 + far_q)
        normalize(0, dilated)

    def plain(initial, last, base):
        total = product(shifted(initial), base + initial)
        for tap in range(initial + 1, last):
            total += product(shifted(tap), base + tap)
        return total

    hooks = {}
    first_plain, centre, second_plain = 9, 18, 19

    tile_copies[0].start()
    tile_copies[1].start()
    own_z(0)
    own_z(1)
    ready = 0
    stage = 0
    for step in range(groups + 3):
        if step < groups:
            z_phase(step)
            if step + 2 < groups:
                own_z(step + 2)
        if step == 1:
            tile_copies[0].wait_recv()
            tile_copies[2].start()
        if 0 <= step - 1 < groups:
            plane_phase(step - 1)
        if 0 <= step - 2 < groups:
            diag_phase(step - 2)
        if step - 3 < 0:
            continue
        core_phase(step - 3)
        ready = (step - 2) * cols
        if stage == 0 and ready >= first_plain:
            first_block()
            stage = 1
        elif stage == 1:
            split = min(ready, centre) - first_plain
            take_halo(0)
            current[...] = radar_ref[...] + plain(0, split, first_plain)
            done = split
            stage = 2
        if stage == 2 and ready > centre:
            current[...] += plain(done, 9, first_plain)
            normalize(1, product(current[...].astype(jnp.bfloat16), centre))
            stage = 3
        elif stage == 3:
            split = min(ready, taps) - second_plain
            take_halo(1)
            current[...] += plain(0, split, second_plain)
            done = split
            stage = 4
        elif stage == 4:
            o_ref[...] = current[...] + plain(done, 9, second_plain)
            stage = 5

    for copy in tile_copies:
        copy.wait_send()
    for g in range(groups):
        pl.when(z < depth - 1)(lambda: z_up(g, z).wait_send())
        pl.when(z > 0)(lambda: z_down(g, z).wait_send())

        def act(source, side, d):
            if side < 0:
                pl.when(z < depth - 1)(lambda: z_up(g, source).wait_send())
            else:
                pl.when(z > 0)(lambda: z_down(g, source).wait_send())
            to_x(g, source).wait_send()
            to_y(g, source).wait_send()
            to_diag(g, source).wait_send()

        others(act)
        for j in range(4):
            to_core(g, j).wait_send()
    for b in range(2):
        for n, (dr, dc, ok) in enumerate(neighbours):
            pl.when(ok)(lambda: halo_copy(b, n).wait_send())


def one_kernel(rows, cols, radar_field, kernels, norm_gain_weights):
    th, tw, channels = radar_field.shape
    part = kernels.shape[-1]
    depth = rows // 2
    flat = jnp.swapaxes(kernels.reshape(BLOCKS * 2, 9, channels, part), 2, 3)
    weights = jnp.concatenate([flat[0], flat[1], flat[2, 4:5], flat[3]])
    taps = weights.shape[0]
    groups = taps // cols
    flat_radar = radar_field.reshape(th * tw, channels)
    vmem = pl.BlockSpec(memory_space=pltpu.VMEM)
    dma = pltpu.SemaphoreType.DMA
    out = pl.pallas_call(
        functools.partial(block_kernel, rows, cols, th, tw, taps),
        out_shape=jax.ShapeDtypeStruct((th * tw, channels), jnp.float32),
        in_specs=[vmem, pl.BlockSpec(memory_space=pl.ANY), vmem, vmem],
        out_specs=vmem,
        scratch_shapes=[
            pltpu.VMEM((taps, depth, 2, part, channels), jnp.bfloat16),
            pltpu.VMEM((3, th * tw, channels), jnp.bfloat16),
            pltpu.VMEM((2, th, tw, channels), jnp.bfloat16),
            pltpu.VMEM((2, 2, th, channels), jnp.bfloat16),
            pltpu.VMEM((2, 2, tw, channels), jnp.bfloat16),
            pltpu.VMEM((2, 2, 3, th, channels), jnp.bfloat16),
            pltpu.VMEM((th + 2, -(-(tw + 2) // 8) * 8, channels), jnp.float32),
            pltpu.VMEM((th * tw, channels), jnp.float32),
            dma((groups,)),
            dma((groups, 4, depth)),
            dma((groups, depth)),
            dma((groups, depth)),
            dma((groups, depth)),
            dma((groups, depth)),
            dma((groups, depth)),
            dma((groups, 4)),
            dma((groups, 4)),
            dma((3,)),
            dma((3,)),
            dma((2, 8)),
            dma((2, 8)),
        ],
        compiler_params=pltpu.CompilerParams(
            collective_id=0, has_side_effects=True, vmem_limit_bytes=48 * 1024 * 1024
        ),
    )(flat_radar.astype(jnp.bfloat16), weights, flat_radar, norm_gain_weights)
    return out.reshape(th, tw, channels)


def solution(mesh):
    rows, cols = mesh.shape["row"], mesh.shape["col"]

    def body(radar_field, kernels, norm_gain_weights):
        if fits(rows, cols, radar_field.shape, kernels.shape):
            return one_kernel(rows, cols, radar_field, kernels, norm_gain_weights)
        return per_device(radar_field, kernels, norm_gain_weights)

    return jax.shard_map(
        body,
        mesh=mesh,
        in_specs=(P("row", "col", None), P(None, None, None, None, None, "row"), P()),
        out_specs=P("row", "col", None),
        check_vma=False,
    )
```

```python
import functools

import jax
import jax.numpy as jnp
from jax import lax
from jax.experimental import pallas as pl
from jax.experimental.pallas import tpu as pltpu
from jax.sharding import PartitionSpec as P

BLOCKS = 2
FIRST_DILATION = 32
SECOND_DILATION = 64


norm_floor = 1e-06


def passed_along(value, axis, steps):
    count = lax.axis_size(axis)
    initial, last = (max(0, -steps), min(count, count - steps))
    return lax.ppermute(value, axis, [(source, source + steps) for source in range(initial, last)])


def extended(cells, sides, width):
    for axis, dim in sides:
        count = lax.axis_size(axis)
        ends = count - 1
        head = lax.slice_in_dim(cells, 0, width, axis=dim)
        tail = lax.slice_in_dim(cells, cells.shape[dim] - width, cells.shape[dim], axis=dim)
        cells = jnp.concatenate(
            [
                lax.ppermute(tail, axis, [(i, (i + 1) % count) for i in range(ends)]),
                cells,
                lax.ppermute(head, axis, [((i + 1) % count, i) for i in range(ends)]),
            ],
            axis=dim,
        )
    return cells


def row_direction(stacked, tap_displacement):
    moved = {}
    for side in (-1, 1):
        moved[side] = passed_along(stacked, "row", -side * tap_displacement)
    return moved


def along_cols(stacked, tap_displacement):
    moved = {}
    for side in (-1, 1):
        moved[side] = passed_along(stacked, "col", -side * tap_displacement)
    return moved


def dilated_taps(cast_state, row_step, col_step):
    tap_list = []
    row_moved = row_direction(cast_state, row_step)
    centre = jnp.stack([row_moved[-1], cast_state, row_moved[1]])
    col_moved = along_cols(centre, col_step)
    for row_off in (-1, 0, 1):
        for col_off in (-1, 0, 1):
            if col_off == 0:
                tap_list.append(centre[row_off + 1])
            else:
                tap_list.append(col_moved[col_off][row_off + 1])
    return jnp.stack(tap_list)


def contract(tap_stack, kernel_part):
    channels = tap_stack.shape[-1]
    flat_taps = tap_stack.reshape(9, -1, channels)
    flat_kernel = kernel_part.reshape(9, channels, -1)
    return lax.dot_general(
        flat_taps, flat_kernel, (((0, 2), (0, 1)), ((), ())), preferred_element_type=jnp.float32
    )


def convolve(tap_stack, kernels, block_index, which):
    gathered = lax.all_gather(kernels[block_index, which], "row", axis=3, tiled=True)
    return contract(tap_stack, gathered)


def per_device(radar_field, kernels, norm_gain_weights):
    tile_rows, tile_cols, channels = radar_field.shape
    dilation_list = [FIRST_DILATION, SECOND_DILATION]
    current = radar_field
    for block_index in range(BLOCKS):
        cast_state = current.astype(jnp.bfloat16)
        spacing = dilation_list[block_index]
        tap_stack = dilated_taps(cast_state, spacing // tile_rows, spacing // tile_cols)
        dilated_output = convolve(tap_stack, kernels, block_index, 0)
        mean_square = jnp.mean(dilated_output * dilated_output, axis=-1, keepdims=True)
        normed = (
            dilated_output / jnp.sqrt(mean_square + norm_floor) * norm_gain_weights[block_index]
        )
        hidden = jax.nn.relu(normed).astype(jnp.bfloat16).reshape(tile_rows, tile_cols, channels)
        padded = extended(hidden, (("row", 0), ("col", 1)), 1)
        plain_taps = []
        for row_off in range(3):
            for col_off in range(3):
                plain_taps.append(
                    padded[row_off : row_off + tile_rows, col_off : col_off + tile_cols]
                )
        plain = convolve(jnp.stack(plain_taps), kernels, block_index, 1)
        current = current + plain.reshape(tile_rows, tile_cols, channels)
    return current


MESH = pl.DeviceIdType.MESH
PLANE = 4
AHEAD, Z_LAG, PLANE_LAG, DIAG_LAG, CORE_LAG = 3, 2, 2, 2, 2
LONG_START, TILE_STEP = 4, 2


def fits(rows, cols, tile, shard):
    height, width = rows * tile[0], cols * tile[1]
    return (
        cols == PLANE
        and rows % 4 == 0
        and height == 2 * FIRST_DILATION
        and width == 2 * FIRST_DILATION
        and SECOND_DILATION >= max(height, width)
        and shard[-1] % 16 == 0
        and tile[1] % 16 == 0
    )


def block_kernel(
    rows, cols, th, tw, taps, parts,
    w_ref, radar_hbm, gain_hbm, o_ref,
    wg, x_ref, gain_ref, xin, hs, ce, rowhalo, colhalo, hp, current,
    load_sem,    local_sem, w_recv, up_send, down_send, x_send, y_send, diag_send, core_send, core_recv, own_send, own_recv,
    tile_send, tile_recv, halo_send, halo_recv,
):
    row, col = lax.axis_index("row"), lax.axis_index("col")
    depth = rows // 2
    groups = taps // cols
    z, core = row // 2, row % 2
    channels = o_ref.shape[-1]
    half = depth // 2
    col_of = [col, col + 1 - 2 * (col % 2), (col + 2) % 4, 3 - col]
    other_core = row + 1 - 2 * core
    far_row = (row + depth) % rows
    far_col = col_of[2]

    def remote(source, target, send, recv, to_row, to_col):
        return pltpu.make_async_remote_copy(
            src_ref=source,
            dst_ref=target,
            send_sem=send,
            recv_sem=recv,
            device_id={"row": to_row, "col": to_col},
            device_id_type=MESH,
        )

    radar_copy = pltpu.make_async_copy(radar_hbm, current, load_sem.at[0])
    gain_copy = pltpu.make_async_copy(gain_hbm, gain_ref, load_sem.at[1])
    radar_copy.start()
    gain_copy.start()
    local_copies = []
    filled = 0
    for n, (conv, first, count) in enumerate(parts):
        source = w_ref.at[conv, pl.ds(first, count)]
        local_copies.append(
            pltpu.make_async_copy(source, wg.at[pl.ds(filled, count), z, core], local_sem.at[n])
        )
        local_copies[-1].start()
        filled += count

    neighbours = []
    for dr in (-1, 0, 1):
        for dc in (-1, 0, 1):
            if dr or dc:
                ok = (row + dr >= 0) & (row + dr < rows) & (col + dc >= 0) & (col + dc < cols)
                neighbours.append((dr, dc, ok))

    barrier = pltpu.get_barrier_semaphore()
    greeted = [
        (z > 0, row - 2, col),
        (z < depth - 1, row + 2, col),
        (None, row, col_of[1]),
        (None, row, col_of[2]),
        (None, other_core, col),
        (None, far_row, col),
    ] + [(ok, row + dr, col + dc) for dr, dc, ok in neighbours]
    expected = 0
    for ok, to_row, to_col in greeted:
        def greet(to_row=to_row, to_col=to_col):
            pl.semaphore_signal(barrier, inc=1, device_id={"row": to_row, "col": to_col}, device_id_type=MESH)

        if ok is None:
            greet()
            expected = expected + 1
        else:
            pl.when(ok)(greet)
            expected = expected + jnp.where(ok, 1, 0)
    hp[...] = jnp.zeros_like(hp)
    radar_copy.wait()
    x_ref[...] = current[...].astype(jnp.bfloat16)
    gain_copy.wait()
    for copy in local_copies:
        copy.wait()
    pl.semaphore_wait(barrier, expected)

    def along_z(g):
        return g == groups - 1

    def tap_of(g, j):
        return cols * g + col_of[j]

    def piece(g, j, source, of=None):
        of = core if of is None else of
        if along_z(g):
            return wg.at[pl.ds(cols * g, cols), source, of]
        return wg.at[tap_of(g, j), source, of]

    def upper_only(g, j):
        return tap_of(g, j) < 3

    def lower_only(g, j):
        return (tap_of(g, j) >= 6) & (tap_of(g, j) < 9)

    def guarded(g, condition, act):
        if cols * g < 9:
            pl.when(condition())(act)
        else:
            act()

    def where_needed(g, j, act):
        def condition():
            return jnp.logical_not((upper_only(g, j) & (z < half)) | (lower_only(g, j) & (z >= half)))

        guarded(g, condition, act)

    def where_comes(g, side, act):
        def condition():
            if side < 0:
                return jnp.logical_not(lower_only(g, 0) & (z >= half))
            return jnp.logical_not(upper_only(g, 0) & (z < half))

        guarded(g, condition, act)

    def pass_up(g, source, act):
        def go():
            guarded(g, lambda: jnp.logical_not(lower_only(g, 0) & (z + 1 >= half)), lambda: act(z_up(g, source)))

        pl.when(z < depth - 1)(go)

    def pass_down(g, source, act):
        def go():
            guarded(g, lambda: jnp.logical_not(upper_only(g, 0) & (z - 1 < half)), lambda: act(z_down(g, source)))

        pl.when(z > 0)(go)

    def z_up(g, source):
        p = piece(g, 0, source)
        return remote(p, p, up_send.at[g, source], w_recv.at[g, 0, source], row + 2, col)

    def z_down(g, source):
        p = piece(g, 0, source)
        return remote(p, p, down_send.at[g, source], w_recv.at[g, 0, source], row - 2, col)

    def to_x(g, source):
        p = piece(g, 0, source)
        return remote(p, p, x_send.at[g, source], w_recv.at[g, 1, source], row, col_of[1])

    def to_y(g, source):
        p = piece(g, 0, source)
        return remote(p, p, y_send.at[g, source], w_recv.at[g, 2, source], row, col_of[2])

    def relay_via(g):
        return 1 if g % 3 == 0 else 2

    def to_diag(g, source):
        via = relay_via(g)
        p = piece(g, via, source)
        return remote(p, p, diag_send.at[g, source], w_recv.at[g, 3, source], row, col_of[3 - via])

    def to_core(g, j, source):
        p = piece(g, j, source)
        return remote(p, p, core_send.at[g, j, source], core_recv.at[g, j, source], other_core, col)

    def own_to_core(g):
        p = wg.at[pl.ds(g * cols, cols), z, core]
        return remote(p, p, own_send.at[g], own_recv.at[g], other_core, col)

    def from_core(g, j, source):
        p = piece(g, j, source, 1 - core)
        remote(p, p, core_send.at[g, j, source], core_recv.at[g, j, source], other_core, col).wait_recv()

    def own_from_core(g):
        p = wg.at[pl.ds(g * cols, cols), z, 1 - core]
        remote(p, p, own_send.at[g], own_recv.at[g], other_core, col).wait_recv()

    def arrived(g, j, source):
        p = piece(g, j, source)
        remote(p, p, x_send.at[g, source], w_recv.at[g, j, source], row, col_of[1]).wait_recv()

    def at_distance(d, act):
        for side in (-1, 1):
            source = z + side * d
            pl.when((source >= 0) & (source < depth))(functools.partial(act, source, side))

    def begin(copy):
        copy.start()

    def end(copy):
        copy.wait_send()

    def own_z(g, act=begin):
        pass_up(g, z, act)
        pass_down(g, z, act)

    def pass_along(g, source, side, act):
        if side < 0:
            pass_up(g, source, act)
        else:
            pass_down(g, source, act)

    def z_phase(g, d):
        def act(source, side):
            def come():
                arrived(g, 0, source)
                pass_along(g, source, side, begin)

                def share():
                    if not along_z(g):
                        to_x(g, source).start()
                        to_y(g, source).start()
                    to_core(g, 0, source).start()

                where_needed(g, 0, share)

            where_comes(g, side, come)

        at_distance(d, act)

    def plane_phase(g, d):
        via = relay_via(g)

        def act(source, side):
            def first():
                arrived(g, via, source)
                to_diag(g, source).start()
                to_core(g, via, source).start()

            def second():
                arrived(g, 3 - via, source)
                to_core(g, 3 - via, source).start()

            where_needed(g, via, first)
            where_needed(g, 3 - via, second)

        at_distance(d, act)

    def diag_phase(g, d):
        def act(source, side):
            def come():
                arrived(g, 3, source)
                to_core(g, 3, source).start()

            where_needed(g, 3, come)

        at_distance(d, act)

    def core_phase(g, d):
        def act(source, side):
            for j in range(1 if along_z(g) else 4):
                where_needed(g, j, lambda j=j: from_core(g, j, source))

        at_distance(d, act)

    def ended(g, d):
        def act(source, side):
            where_comes(g, side, lambda: pass_along(g, source, side, end))

            def shared():
                if not along_z(g):
                    to_x(g, source).wait_send()
                    to_y(g, source).wait_send()
                to_core(g, 0, source).wait_send()

            where_needed(g, 0, shared)
            if along_z(g):
                return
            via = relay_via(g)
            where_needed(g, via, lambda: to_diag(g, source).wait_send())
            for j in range(1, 4):
                where_needed(g, j, lambda j=j: to_core(g, j, source).wait_send())

        at_distance(d, act)

    tile_copies = [
        remote(x_ref, xin.at[0], tile_send.at[0], tile_recv.at[0], far_row, col),
        remote(x_ref, xin.at[1], tile_send.at[1], tile_recv.at[1], row, far_col),
        remote(xin.at[0], xin.at[2], tile_send.at[2], tile_recv.at[2], row, far_col),
    ]

    def product(cells, tap):
        weight = wg[tap].reshape(channels, channels)
        return lax.dot_general(cells, weight, (((1,), (1,)), ((), ())), preferred_element_type=jnp.float32)

    def halo_copy(b, n):
        dr, dc, _ = neighbours[n]
        if dc == 0:
            source = hs.at[b, 0 if dr < 0 else th - 1]
            target = rowhalo.at[b, 1 if dr < 0 else 0]
        else:
            source = ce.at[b, 0 if dc < 0 else 1]
            target = colhalo.at[b, 1 if dc < 0 else 0, 1 - dr]
        return remote(source, target, halo_send.at[b, n], halo_recv.at[b, 7 - n], row + dr, col + dc)

    def halo_arrived(b, n):
        dr, dc, _ = neighbours[n]
        if dc == 0:
            target = rowhalo.at[b, 0 if dr < 0 else 1]
        else:
            target = colhalo.at[b, 0 if dc < 0 else 1, dr + 1]
        remote(target, target, halo_send.at[b, n], halo_recv.at[b, n], row + dr, col + dc).wait_recv()

    def normalize(b, dilated):
        mean_square = jnp.mean(dilated * dilated, axis=-1, keepdims=True)
        normed = dilated / jnp.sqrt(mean_square + norm_floor) * gain_ref[b : b + 1, :]
        hidden = jax.nn.relu(normed).astype(jnp.bfloat16).reshape(th, tw, channels)
        hs[b] = hidden
        wide = hidden.astype(jnp.float32)
        ce[b, 0] = wide[:, 0, :].astype(jnp.bfloat16)
        ce[b, 1] = wide[:, tw - 1, :].astype(jnp.bfloat16)
        hp[1 : th + 1, 1 : tw + 1, :] = wide
        for n, (dr, dc, ok) in enumerate(neighbours):
            pl.when(ok)(lambda n=n: halo_copy(b, n).start())

    def take_halo(b):
        for n, (dr, dc, ok) in enumerate(neighbours):
            def act(n=n, dr=dr, dc=dc):
                halo_arrived(b, n)
                to_row = 0 if dr < 0 else th + 1
                to_col = 0 if dc < 0 else tw + 1
                if dc == 0:
                    hp[to_row, 1 : tw + 1, :] = rowhalo[b, 0 if dr < 0 else 1].astype(jnp.float32)
                else:
                    edge = colhalo[b, 0 if dc < 0 else 1, dr + 1].astype(jnp.float32)
                    if dr == 0:
                        hp[1 : th + 1, to_col : to_col + 1, :] = edge.reshape(th, 1, channels)
                    else:
                        at = th - 1 if dr < 0 else 0
                        hp[to_row, to_col : to_col + 1, :] = edge[at : at + 1, :]

            pl.when(ok)(act)

    def shifted(tap):
        p, q = tap // 3, tap % 3
        return hp[p : p + th, q : q + tw, :].astype(jnp.bfloat16).reshape(th * tw, channels)

    def first_block():
        tile_copies[1].wait_recv()
        tile_copies[2].wait_recv()
        far_p = jnp.where(row < depth, 2, 0)
        far_q = jnp.where(col < cols // 2, 2, 0)
        dilated = product(x_ref[...], 4)
        dilated += product(xin[0], far_p * 3 + 1)
        dilated += product(xin[1], 3 + far_q)
        dilated += product(xin[2], far_p * 3 + far_q)
        normalize(0, dilated)

    def plain(initial, last, base):
        total = product(shifted(initial), base + initial)
        for tap in range(initial + 1, last):
            total += product(shifted(tap), base + tap)
        return total

    hooks = {}
    first_plain, centre, second_plain = 9, 18, 19

    long = groups - 1
    long_at = [LONG_START + Z_LAG * n for n in range(depth)]
    own_z(0)
    tile_copies[1].start()
    own_z(1)
    tile_copies[0].start()
    for g in range(2, AHEAD):
        own_z(g)
    ready = 0
    stage = 0
    for g in range(groups):
        own_to_core(g).start()
    delays = (0, PLANE_LAG, PLANE_LAG + DIAG_LAG, PLANE_LAG + DIAG_LAG + CORE_LAG)
    whole_lag = Z_LAG * (depth - 2) + delays[-1]
    for step in range(long + whole_lag):
        for lag, phase in zip(delays, (z_phase, plane_phase, diag_phase, core_phase)):
            for d in range(1, depth):
                g = step - lag - Z_LAG * (d - 1)
                if 0 <= g < long:
                    phase(g, d)
            if lag == 0:
                if step + AHEAD < long:
                    own_z(step + AHEAD)
                if step == max(LONG_START - 2, 0):
                    own_z(long)
                for d in range(1, depth):
                    if step == long_at[d - 1]:
                        z_phase(long, d)
                    if step == long_at[d - 1] + CORE_LAG:
                        core_phase(long, d)
        if step == TILE_STEP:
            tile_copies[0].wait_recv()
            tile_copies[2].start()
        whole = step - whole_lag
        if whole < 0:
            continue
        own_from_core(whole)
        ready = (whole + 1) * cols
        if whole == long - 1:
            own_from_core(long)
            ready = taps
        if stage == 0 and ready >= first_plain:
            first_block()
            stage = 1
        elif stage == 1:
            done = min(ready, centre) - first_plain
            take_halo(0)
            current[...] += plain(0, done, first_plain)
            stage = 2
        if stage == 2 and ready > centre:
            if done < 9:
                current[...] += plain(done, 9, first_plain)
            normalize(1, product(current[...].astype(jnp.bfloat16), centre))
            stage = 3
    take_halo(1)
    o_ref[...] = current[...] + plain(0, 9, second_plain)

    for copy in tile_copies:
        copy.wait_send()
    for g in range(groups):
        own_z(g, end)
        for d in range(1, depth):
            ended(g, d)
        own_to_core(g).wait_send()
    for b in range(2):
        for n, (dr, dc, ok) in enumerate(neighbours):
            pl.when(ok)(lambda: halo_copy(b, n).wait_send())


def one_kernel(rows, cols, radar_field, kernels, norm_gain_weights):
    th, tw, channels = radar_field.shape
    part = kernels.shape[-1]
    depth = rows // 2
    flat = jnp.swapaxes(kernels.reshape(BLOCKS * 2, 9, channels, part), 2, 3)
    weights = flat
    parts = ((0, 0, 9), (1, 0, 9), (2, 4, 1), (3, 0, 9))
    taps = sum(count for _, _, count in parts)
    groups = taps // cols
    flat_radar = radar_field.reshape(th * tw, channels)
    vmem = pl.BlockSpec(memory_space=pltpu.VMEM)
    dma = pltpu.SemaphoreType.DMA
    out = pl.pallas_call(
        functools.partial(block_kernel, rows, cols, th, tw, taps, parts),
        out_shape=jax.ShapeDtypeStruct((th * tw, channels), jnp.float32),
        in_specs=[pl.BlockSpec(memory_space=pltpu.HBM)] * 3,
        out_specs=vmem,
        scratch_shapes=[
            pltpu.VMEM((taps, depth, 2, part, channels), jnp.bfloat16),
            pltpu.VMEM((th * tw, channels), jnp.bfloat16),
            pltpu.VMEM(norm_gain_weights.shape, jnp.float32),
            pltpu.VMEM((3, th * tw, channels), jnp.bfloat16),
            pltpu.VMEM((2, th, tw, channels), jnp.bfloat16),
            pltpu.VMEM((2, 2, th, channels), jnp.bfloat16),
            pltpu.VMEM((2, 2, tw, channels), jnp.bfloat16),
            pltpu.VMEM((2, 2, 3, th, channels), jnp.bfloat16),
            pltpu.VMEM((th + 2, -(-(tw + 2) // 8) * 8, channels), jnp.float32),
            pltpu.VMEM((th * tw, channels), jnp.float32),
            dma((2,)),
            dma((len(parts),)),
            dma((groups, 4, depth)),
            dma((groups, depth)),
            dma((groups, depth)),
            dma((groups, depth)),
            dma((groups, depth)),
            dma((groups, depth)),
            dma((groups, 4, depth)),
            dma((groups, 4, depth)),
            dma((groups,)),
            dma((groups,)),
            dma((3,)),
            dma((3,)),
            dma((2, 8)),
            dma((2, 8)),
        ],
        compiler_params=pltpu.CompilerParams(
            collective_id=0, has_side_effects=True, vmem_limit_bytes=67_000_000
        ),
    )(weights, flat_radar, norm_gain_weights)
    return out.reshape(th, tw, channels)


def solution(mesh):
    rows, cols = mesh.shape["row"], mesh.shape["col"]

    def body(radar_field, kernels, norm_gain_weights):
        if fits(rows, cols, radar_field.shape, kernels.shape):
            return one_kernel(rows, cols, radar_field, kernels, norm_gain_weights)
        return per_device(radar_field, kernels, norm_gain_weights)

    return jax.shard_map(
        body,
        mesh=mesh,
        in_specs=(P("row", "col", None), P(None, None, None, None, None, "row"), P()),
        out_specs=P("row", "col", None),
        check_vma=False,
    )
```
